512 devices in a mesh: gx: 8 (over x, y_hi), gy: 8 (over z), gz: 8 (over y_lo, core).
Axes of the slice: x: 4, y: 8 (y_hi: 2, y_lo: 4; y = y_hi * 4 + y_lo), z: 8, core: 2. Of those that a mesh axis runs over, the one named last changes fastest.
Arguments:
- orbitals: float32 [128, 128, 128, 64], P('gx', 'gy', 'gz'), may hold values from -6 to 6
- potential: float32 [128, 128, 128], P('gx', 'gy', 'gz'), may hold values from -1.5 to 1
Outputs:
- basis: float32 [128, 128, 128, 64], P('gx', 'gy', 'gz')
- blocks: float32 [8, 8, 8, 7, 64, 64], P('gx', 'gy', 'gz')
The draws below stay inside these ranges and needn't reach their ends.
All inputs are finite; a program needn't handle non-finite values.
Results may differ from the reference program's by a relative error of at most 0.0003.
Values sent between devices are 32-bit elements; how exact they have to be, the bound alone decides.
A program may use at most 128 MiB of HBM per device.

```python
import jax
import jax.numpy as jnp
import numpy as np
from jax import lax

ORBITALS = 64
CELLS = 16
BUF = 3
DEGREE = 2
EXT = 22
NX = 128
NY = 128
NZ = 128
N_GX = 8
N_GY = 8
N_GZ = 8


def block_scale(key, extent, pieces, low, top_value):
    def one(dim, parts):
        draws = jax.random.uniform(jax.random.fold_in(jax.random.fold_in(key, 6), dim), (parts,), jnp.float32, low / len(pieces), top_value / len(pieces))
        return jnp.repeat(jnp.exp(draws), extent[dim] // parts).reshape((-1,) + (1,) * (len(extent) - dim - 1))

    loudness = one(*pieces[0])
    for cut in pieces[1:]:
        loudness = loudness * one(*cut)
    return loudness


def noise(own_key, dims, deviation, limit, shards=(), kind=jnp.bfloat16):
    drawn = deviation * jax.random.normal(own_key, dims, jnp.float32)
    if shards:
        drawn = drawn * block_scale(own_key, dims, shards, -0.22, 0.18)
    return jnp.clip(drawn, -limit, limit).astype(kind)


def setup_inputs(seed: int = 0) -> dict:
    splits = jax.random.split(jax.random.key(seed), 3)
    orbitals = noise(splits[0], (NX, NY, NZ, ORBITALS), 1.0, 6.0, ((0, 8), (1, 8), (2, 8)), jnp.float32)
    potential = jnp.clip(-1.5 + 2.5 * jax.random.uniform(splits[1], (NX, NY, NZ), jnp.float32) ** block_scale(splits[1], (NX, NY, NZ), ((0, 8), (1, 8), (2, 8)), -0.2, 0.2), -1.5, 1.0)
    return dict(orbitals=orbitals, potential=potential)


PENALTY = 2.0
LOW_BOUND = -1.5
CUTOFF = 8.0
HIGH_BOUND = 16.0


def spectral_tables(points):
    indices = np.arange(points)
    offsets = indices[:, None] - indices[None, :]
    nyquist = points // 2
    deriv_one = np.zeros((points, points))
    deriv_two = np.zeros((points, points))
    for harmonic in range(1, nyquist):
        wavenum = 2.0 * np.pi * harmonic / points
        deriv_one = deriv_one - 2.0 * wavenum * np.sin(wavenum * offsets) / points
        deriv_two = deriv_two - 2.0 * wavenum * wavenum * np.cos(wavenum * offsets) / points
    deriv_two = deriv_two - np.pi * np.pi * np.cos(np.pi * offsets) / points
    return jnp.asarray(deriv_one, jnp.float32), jnp.asarray(deriv_two, jnp.float32)


def apply_along(matrix, field, axis_pos):
    forms = ("ia,ajko->ijko", "ja,iako->ijko", "ka,ijao->ijko")
    return jnp.einsum(forms[axis_pos], matrix, field, precision=lax.Precision.HIGHEST)


def hamiltonian(field, ext_pot, deriv_two):
    laplace = apply_along(deriv_two, field, 0) + apply_along(deriv_two, field, 1)
    laplace = laplace + apply_along(deriv_two, field, 2)
    return -0.5 * laplace + ext_pot[..., None] * field


def chebyshev(start, ext_pot, deriv_two, degree):
    half_width = (HIGH_BOUND - CUTOFF) / 2.0
    center = (HIGH_BOUND + CUTOFF) / 2.0
    scale_now = half_width / (LOW_BOUND - center)
    tau_factor = 2.0 / scale_now
    previous = start
    current = (hamiltonian(start, ext_pot, deriv_two) - center * start) * (scale_now / half_width)
    for iteration in range(1, degree):
        scale_next = 1.0 / (tau_factor - scale_now)
        applied = hamiltonian(current, ext_pot, deriv_two) - center * current
        following = applied * (2.0 * scale_next / half_width) - (scale_now * scale_next) * previous
        previous = current
        current = following
        scale_now = scale_next
    return current


def element_fields(ext_orb, ext_pot, deriv_one, deriv_two, margin, cells, degree):
    filtered = chebyshev(ext_orb, ext_pot, deriv_two, degree)
    stop = margin + cells
    row_block = deriv_one[margin:stop]
    interior = filtered[margin:stop, margin:stop, margin:stop]
    grad_x = apply_along(row_block, filtered[:, margin:stop, margin:stop], 0)
    grad_y = apply_along(row_block, filtered[margin:stop, :, margin:stop], 1)
    grad_z = apply_along(row_block, filtered[margin:stop, margin:stop, :], 2)
    return interior, grad_x, grad_y, grad_z


def face_product(left, right):
    return jnp.einsum("...pqi,...pqj->...ij", left, right, precision=lax.Precision.HIGHEST)


def neighbour_block(own_value, own_deriv, other_value, other_deriv, sign):
    skew = face_product(own_deriv, other_value) - face_product(own_value, other_deriv)
    return 0.25 * sign * skew - 0.5 * PENALTY * face_product(own_value, other_value)


def own_face(value, deriv, sign):
    mixed = face_product(value, deriv) + face_product(deriv, value)
    return -0.25 * sign * mixed + 0.5 * PENALTY * face_product(value, value)


def assemble(interior, gradients, pot_el, lowers, uppers):
    volume_form = "...xyzi,...xyzj->...ij"
    diagonal = jnp.einsum(volume_form, interior, pot_el[..., None] * interior, precision=lax.Precision.HIGHEST)
    for axis_pos in range(3):
        diagonal = diagonal + 0.5 * jnp.einsum(volume_form, gradients[axis_pos], gradients[axis_pos], precision=lax.Precision.HIGHEST)
    cells = interior.shape[-2]
    coupled = []
    for axis_pos in range(3):
        grid_axis = interior.ndim - 4 + axis_pos
        low_value = jnp.take(interior, 0, axis=grid_axis)
        low_deriv = jnp.take(gradients[axis_pos], 0, axis=grid_axis)
        high_value = jnp.take(interior, cells - 1, axis=grid_axis)
        high_deriv = jnp.take(gradients[axis_pos], cells - 1, axis=grid_axis)
        diagonal = diagonal + own_face(low_value, low_deriv, -1.0)
        diagonal = diagonal + own_face(high_value, high_deriv, 1.0)
        coupled.append(neighbour_block(low_value, low_deriv, lowers[axis_pos][0], lowers[axis_pos][1], -1.0))
        coupled.append(neighbour_block(high_value, high_deriv, uppers[axis_pos][0], uppers[axis_pos][1], 1.0))
    return jnp.stack([diagonal] + coupled, axis=-3)


def reference(orbitals, potential):
    deriv_one, deriv_two = spectral_tables(EXT)
    offsets = jnp.arange(EXT, dtype=jnp.int32) - BUF

    def one_element(flat_index):
        elem_x = flat_index // (N_GY * N_GZ)
        elem_y = (flat_index // N_GZ) % N_GY
        elem_z = flat_index % N_GZ
        rows_x = ((elem_x * CELLS + offsets) % NX).astype(jnp.int32)
        rows_y = ((elem_y * CELLS + offsets) % NY).astype(jnp.int32)
        rows_z = ((elem_z * CELLS + offsets) % NZ).astype(jnp.int32)
        ext_orb = jnp.take(jnp.take(jnp.take(orbitals, rows_x, axis=0), rows_y, axis=1), rows_z, axis=2)
        ext_pot = jnp.take(jnp.take(jnp.take(potential, rows_x, axis=0), rows_y, axis=1), rows_z, axis=2)
        return element_fields(ext_orb, ext_pot, deriv_one, deriv_two, BUF, CELLS, DEGREE)

    fields = lax.map(one_element, jnp.arange(N_GX * N_GY * N_GZ, dtype=jnp.int32))
    full_shape = (N_GX, N_GY, N_GZ, CELLS, CELLS, CELLS, ORBITALS)
    interior = fields[0].reshape(full_shape)
    gradients = (fields[1].reshape(full_shape), fields[2].reshape(full_shape), fields[3].reshape(full_shape))
    pot_el = potential.reshape(N_GX, CELLS, N_GY, CELLS, N_GZ, CELLS).transpose(0, 2, 4, 1, 3, 5)
    lowers = []
    uppers = []
    for axis_pos in range(3):
        grid_axis = 3 + axis_pos
        lowers.append((jnp.roll(jnp.take(interior, CELLS - 1, axis=grid_axis), 1, axis=axis_pos),
                       jnp.roll(jnp.take(gradients[axis_pos], CELLS - 1, axis=grid_axis), 1, axis=axis_pos)))
        uppers.append((jnp.roll(jnp.take(interior, 0, axis=grid_axis), -1, axis=axis_pos),
                       jnp.roll(jnp.take(gradients[axis_pos], 0, axis=grid_axis), -1, axis=axis_pos)))
    blocks = assemble(interior, gradients, pot_el, lowers, uppers)
    basis = interior.transpose(0, 3, 1, 4, 2, 5, 6).reshape(NX, NY, NZ, ORBITALS)
    return basis, blocks
```

```python
import functools

import jax
import jax.numpy as jnp
import numpy as np
from jax import lax
from jax.experimental import pallas as pl
from jax.experimental.pallas import tpu as pltpu
from jax.sharding import PartitionSpec as P

BUF = 3
CELLS = 16
EXT = 22
ORB = 64
HALF = EXT // 2
PENALTY = 2.0
LOW_BOUND = -1.5
CUTOFF = 8.0
HIGH_BOUND = 16.0

YLO, YHI, ZLO, ZHI, ROWS = 256, 304, 352, 424, 496
ZPAD = 24
MESSAGE = 392
AXES = ("gx", "gy", "gz")
MESH = pl.DeviceIdType.MESH
F32 = jnp.float32
BF16 = jnp.bfloat16


def spectral_tables(points):
    indices = np.arange(points)
    offsets = indices[:, None] - indices[None, :]
    nyquist = points // 2
    deriv_one = np.zeros((points, points))
    deriv_two = np.zeros((points, points))
    for harmonic in range(1, nyquist):
        wavenum = 2.0 * np.pi * harmonic / points
        deriv_one = deriv_one - 2.0 * wavenum * np.sin(wavenum * offsets) / points
        deriv_two = deriv_two - 2.0 * wavenum * wavenum * np.cos(wavenum * offsets) / points
    deriv_two = deriv_two - np.pi * np.pi * np.cos(np.pi * offsets) / points
    return deriv_one, deriv_two


def row_cells():
    cells = [(-1, -1)] * ROWS
    for y in range(CELLS):
        for z in range(CELLS):
            cells[y * CELLS + z] = (BUF + y, BUF + z)
    for h in range(BUF):
        for z in range(CELLS):
            cells[YLO + h * CELLS + z] = (h, BUF + z)
            cells[YHI + h * CELLS + z] = (BUF + CELLS + h, BUF + z)
        for k in range(EXT):
            y = BUF + k if k < CELLS else (k - CELLS if k < CELLS + BUF else k)
            cells[ZLO + h * ZPAD + k] = (y, h)
            cells[ZHI + h * ZPAD + k] = (y, BUF + CELLS + h)
    return np.array(cells)


def split_host(matrix):
    full = jnp.asarray(matrix, F32)
    high = full.astype(BF16)
    low = (full - high.astype(F32)).astype(BF16)
    return jnp.concatenate([high, low, high], axis=1)


def plane_matrices():
    deriv_one, deriv_two = spectral_tables(EXT)
    cells = row_cells()
    real = (cells[:, 0] >= 0).astype(np.float64)
    ys, zs = np.maximum(cells[:, 0], 0), np.maximum(cells[:, 1], 0)
    same_y = (ys[:, None] == ys[None, :]) * real[:, None] * real[None, :]
    same_z = (zs[:, None] == zs[None, :]) * real[:, None] * real[None, :]
    kinetic = -0.5 * (same_z * deriv_two[ys[:, None], ys[None, :]] + same_y * deriv_two[zs[:, None], zs[None, :]])
    grad_y = (same_z * deriv_one[ys[:, None], ys[None, :]])[:YLO]
    grad_z = (same_y * deriv_one[zs[:, None], zs[None, :]])[:YLO]
    return split_host(kinetic), split_host(np.concatenate([grad_y, grad_z], axis=0))


def pair_coefs():
    deriv_one, deriv_two = spectral_tables(EXT)
    second = np.zeros((16, 128))
    first = np.zeros((16, 128))
    for d in range(HALF):
        for table, out, factor in ((deriv_two, second, -0.25), (deriv_one, first, 0.5)):
            near, far = table[d, 0], table[(d + HALF) % EXT, 0]
            out[d, :ORB] = factor * (near + far)
            out[d, ORB:] = factor * (near - far)
    return jnp.asarray(np.concatenate([second, first]), F32)


def cheb_constants():
    half_width = (HIGH_BOUND - CUTOFF) / 2.0
    center = (HIGH_BOUND + CUTOFF) / 2.0
    scale_now = half_width / (LOW_BOUND - center)
    scale_next = 1.0 / (2.0 / scale_now - scale_now)
    return center, scale_now / half_width, 2.0 * scale_next / half_width, scale_now * scale_next


def split(value):
    high = value.astype(BF16)
    return high, (value - high.astype(F32)).astype(BF16)


def stacked(value):
    high, low = split(value)
    return jnp.concatenate([high, high, low], axis=0)


def swap(value):
    return pltpu.roll(value, ORB, 1)


def matmul(left, right):
    return jnp.dot(left, right, preferred_element_type=F32)


def gram(left, right):
    return lax.dot_general(left, right, (((0,), (0,)), ((), ())), preferred_element_type=F32)


def gram_split(left, right):
    (lh, ll), (rh, rl) = left, right
    return gram(lh, rh) + (gram(lh, rl) + gram(ll, rh))


def left_lanes(rows):
    return lax.broadcasted_iota(jnp.int32, (rows, 128), 1) < ORB


def kernel(
    x_ref, pot_ref, kin_ref, grad_ref, coef_ref,
    basis_ref, blocks_ref,
    xs, xr, pot_s, cells, pots, work, filt, zs, gx, gyz, faces, others,
    xsend, xrecv, ysend, yrecv, zsend, zrecv, fsend, frecv,
):
    center, alpha, beta, gamma = cheb_constants()
    me = [lax.axis_index(a) for a in AXES]
    size = [lax.axis_size(a) for a in AXES]

    def beside(axis, step):
        return {AXES[axis]: lax.rem(me[axis] + step + size[axis], size[axis])}

    barrier = pltpu.get_barrier_semaphore()
    for axis in range(3):
        for step in (-1, 1):
            pl.semaphore_signal(barrier, inc=1, device_id=beside(axis, step), device_id_type=MESH)

    def send(src, dst, ssem, rsem, axis, step):
        copy = pltpu.make_async_remote_copy(
            src_ref=src, dst_ref=dst, send_sem=ssem, recv_sem=rsem,
            device_id=beside(axis, step), device_id_type=MESH,
        )
        copy.start()
        return copy

    for side, start in ((0, 0), (1, CELLS - BUF)):
        for j in range(BUF):
            xs[side, j * 128 : (j + 1) * 128, :] = jnp.concatenate(
                [x_ref[start + j, :8].reshape(128, ORB), x_ref[start + j, 8:].reshape(128, ORB)], axis=1
            )
    xs[0, 384:392, :] = pot_ref[0:8, :]
    xs[1, 384:392, :] = pot_ref[24:32, :]
    zs[...] = jnp.zeros_like(zs)
    pl.semaphore_wait(barrier, 6)
    xcopies = [
        send(xs.at[0], xr.at[0], xsend.at[0], xrecv.at[0], 0, -1),
        send(xs.at[1], xr.at[1], xsend.at[1], xrecv.at[1], 0, 1),
    ]

    zero = jnp.zeros((256, ORB), F32)
    for a in range(HALF):
        low = x_ref[a - BUF].reshape(256, ORB) if a >= BUF else zero
        high = x_ref[a + 8].reshape(256, ORB) if a < 8 else zero
        cells[a, :256, :] = jnp.concatenate([low, high], axis=1)
    for copy in xcopies:
        copy.wait()
    keep = left_lanes(128)
    for j in range(BUF):
        got = xr[1, j * 128 : (j + 1) * 128, :]
        cells[j, 0:128, :] = jnp.where(keep, got, cells[j, 0:128, :])
        cells[j, 128:256, :] = jnp.where(keep, swap(got), cells[j, 128:256, :])
        got = xr[0, j * 128 : (j + 1) * 128, :]
        cells[8 + j, 0:128, :] = jnp.where(keep, cells[8 + j, 0:128, :], swap(got))
        cells[8 + j, 128:256, :] = jnp.where(keep, cells[8 + j, 128:256, :], got)
    pot_s[0:6, :] = xr[1, 386:392, :]
    pot_s[6:38, :] = pot_ref[...]
    pot_s[38:44, :] = xr[0, 384:390, :]
    pot_s[44:48, :] = jnp.zeros((4, 128), F32)
    for h in range(2):
        part = jnp.concatenate([pot_s[pl.ds(h, 24, stride=2), :], jnp.zeros((104, 128), F32)], axis=0)
        cells[HALF, h * 128 : (h + 1) * 128, :] = part.T

    ycopies = [
        send(cells.at[:, 0:48, :], cells.at[:, YHI : YHI + 48, :], ysend.at[0], yrecv.at[0], 1, -1),
        send(cells.at[:, 208:256, :], cells.at[:, YLO : YLO + 48, :], ysend.at[1], yrecv.at[1], 1, 1),
    ]
    for copy in ycopies:
        copy.wait()

    @pl.loop(0, HALF + 1)
    def _(a):
        for side, start in ((0, 0), (1, CELLS - BUF)):
            for h in range(BUF):
                zs[side, a, h * ZPAD : h * ZPAD + EXT, :] = cells[a, pl.ds(start + h, EXT, stride=CELLS), :]

    zcopies = [
        send(zs.at[0], cells.at[:, ZHI : ZHI + 72, :], zsend.at[0], zrecv.at[0], 2, -1),
        send(zs.at[1], cells.at[:, ZLO : ZLO + 72, :], zsend.at[1], zrecv.at[1], 2, 1),
    ]
    for copy in zcopies:
        copy.wait()

    sign = jnp.where(left_lanes(8), 1.0, -1.0).astype(F32)

    def along_x(planes, base, odd, out):
        coefs = [jnp.broadcast_to(coef_ref[base + d : base + d + 1, :], (8, 128)) for d in range(HALF)]
        mixed = [swap(v) + sign * v for v in planes]
        for a in range(HALF):
            total = None
            for b in range(HALF):
                if odd and a == b:
                    continue
                term = coefs[abs(a - b)] * mixed[b]
                if total is None:
                    total = term if not (odd and a < b) else -term
                else:
                    total = total - term if odd and a < b else total + term
            out(a, swap(total) + sign * total)

    @pl.loop(0, ROWS // 8)
    def _(r):
        rows = pl.ds(pl.multiple_of(r * 8, 8), 8)
        planes = [cells[a, rows, :] for a in range(HALF)]
        column = cells[HALF, rows, :]
        keep8 = left_lanes(8)

        def out(a, value):
            pot = jnp.where(
                keep8,
                jnp.broadcast_to(column[:, a : a + 1], (8, 128)),
                jnp.broadcast_to(column[:, a + HALF : a + HALF + 1], (8, 128)),
            )
            pots[a, rows, :] = pot
            work[a, rows, :] = value + (pot - center) * planes[a]

        along_x(planes, 0, False, out)

    work[HALF] = jnp.zeros((ROWS, 128), F32)

    @pl.loop(0, 6)
    def _(g):
        pair = jnp.concatenate([cells[2 * g], cells[2 * g + 1]], axis=1)
        done = matmul(kin_ref[...], stacked(pair))
        work[2 * g] = work[2 * g] + done[:, :128]
        work[2 * g + 1] = work[2 * g + 1] + done[:, 128:]

    @pl.loop(0, ROWS // 8)
    def _(r):
        rows = pl.ds(pl.multiple_of(r * 8, 8), 8)
        planes = [work[a, rows, :] for a in range(HALF)]

        def out(a, value):
            applied = value + (pots[a, rows, :] - center) * planes[a]
            filt[a, rows, :] = (alpha * beta) * applied - gamma * cells[a, rows, :]

        along_x(planes, 0, False, out)

    filt[HALF] = jnp.zeros((ROWS, 128), F32)

    @pl.loop(0, 6)
    def _(g):
        pair = jnp.concatenate([work[2 * g], work[2 * g + 1]], axis=1)
        done = (alpha * beta) * matmul(kin_ref[...], stacked(pair))
        filt[2 * g] = filt[2 * g] + done[:, :128]
        filt[2 * g + 1] = filt[2 * g + 1] + done[:, 128:]

    @pl.loop(0, 32)
    def _(r):
        rows = pl.ds(pl.multiple_of(r * 8, 8), 8)
        planes = [filt[a, rows, :] for a in range(HALF)]

        def out(a, value):
            gx[a, rows, :] = value

        along_x(planes, 16, True, out)

    keep256 = left_lanes(256)
    faces[0] = jnp.where(keep256, filt[3, :256, :], swap(gx[3]))
    faces[1] = jnp.where(keep256, swap(filt[7, :256, :]), gx[7])
    fcopies = [
        send(faces.at[0], others.at[1], fsend.at[0], frecv.at[1], 0, -1),
        send(faces.at[1], others.at[0], fsend.at[1], frecv.at[0], 0, 1),
    ]

    @pl.loop(0, 6)
    def _(g):
        pair = jnp.concatenate([filt[2 * g], filt[2 * g + 1]], axis=1)
        done = matmul(grad_ref[...], stacked(pair))
        gyz[2 * g] = done[:, :128]
        gyz[2 * g + 1] = done[:, 128:]

    keep16 = left_lanes(16)
    for i in range(CELLS):
        a, lower = (i + BUF, True) if i < 8 else (i - 8, False)
        for side, layer in ((0, 0), (1, CELLS - 1)):
            value = filt[a, layer * 16 : layer * 16 + 16, :]
            deriv = gyz[a, layer * 16 : layer * 16 + 16, :]
            faces[2 + side, i * 16 : i * 16 + 16, :] = (
                jnp.where(keep16, value, swap(deriv)) if lower else jnp.where(keep16, swap(value), deriv)
            )
            value = filt[a, pl.ds(layer, 16, stride=16), :]
            deriv = gyz[a, pl.ds(256 + layer, 16, stride=16), :]
            faces[4 + side, i * 16 : i * 16 + 16, :] = (
                jnp.where(keep16, value, swap(deriv)) if lower else jnp.where(keep16, swap(value), deriv)
            )
    for axis in (1, 2):
        fcopies.append(send(faces.at[2 * axis], others.at[2 * axis + 1], fsend.at[2 * axis], frecv.at[2 * axis + 1], axis, -1))
        fcopies.append(send(faces.at[2 * axis + 1], others.at[2 * axis], fsend.at[2 * axis + 1], frecv.at[2 * axis], axis, 1))

    for i in range(CELLS):
        a, lower = (i + BUF, True) if i < 8 else (i - 8, False)
        value = filt[a, :256, :]
        value = value[:, :ORB] if lower else swap(value)[:, :ORB]
        basis_ref[i] = value.reshape(16, 16, ORB)

    def volume(a, total):
        inside = jnp.where(keep256, (a >= BUF).astype(F32), (a < 8).astype(F32))
        value = filt[a, :256, :]
        mass = gram_split(split(value), split(inside * pots[a, :256, :] * value))
        square = jnp.zeros((128, 128), F32)
        for part in (gx[a], gyz[a, :256, :], gyz[a, 256:, :]):
            high, low = split(inside * part)
            square = square + (gram(high, high) + gram(high, low) + gram(low, high))
        return total + mass + 0.5 * square

    total = lax.fori_loop(0, HALF, volume, jnp.zeros((128, 128), F32))
    diagonal = total[:ORB, :ORB] + total[ORB:, ORB:]
    for f in range(6):
        s = -1.0 if f % 2 == 0 else 1.0
        pair = split(faces[f])
        own = gram_split(pair, pair)
        diagonal = diagonal - (0.25 * s) * (own[:ORB, ORB:] + own[ORB:, :ORB]) + (0.5 * PENALTY) * own[:ORB, :ORB]
    blocks_ref[0] = diagonal
    for f in (2, 3, 4, 5, 0, 1):
        fcopies[f ^ 1].wait_recv()
        s = -1.0 if f % 2 == 0 else 1.0
        both = gram_split(split(faces[f]), split(others[f]))
        blocks_ref[1 + f] = (0.25 * s) * (both[ORB:, :ORB] - both[:ORB, ORB:]) - (0.5 * PENALTY) * both[:ORB, :ORB]
    for copy in fcopies:
        copy.wait_send()


def on_device(orbitals, potential):
    kinetic, gradient = plane_matrices()
    vmem = pl.BlockSpec(memory_space=pltpu.VMEM)
    dma = pltpu.SemaphoreType.DMA
    basis, blocks = pl.pallas_call(
        kernel,
        out_shape=(
            jax.ShapeDtypeStruct((CELLS, CELLS, CELLS, ORB), F32),
            jax.ShapeDtypeStruct((7, ORB, ORB), F32),
        ),
        in_specs=[vmem] * 5,
        out_specs=(vmem, vmem),
        scratch_shapes=[
            pltpu.VMEM((2, MESSAGE, 128), F32),
            pltpu.VMEM((2, MESSAGE, 128), F32),
            pltpu.VMEM((48, 128), F32),
            pltpu.VMEM((12, ROWS, 128), F32),
            pltpu.VMEM((HALF, ROWS, 128), F32),
            pltpu.VMEM((12, ROWS, 128), F32),
            pltpu.VMEM((12, ROWS, 128), F32),
            pltpu.VMEM((2, 12, 72, 128), F32),
            pltpu.VMEM((HALF, 256, 128), F32),
            pltpu.VMEM((12, 512, 128), F32),
            pltpu.VMEM((6, 256, 128), F32),
            pltpu.VMEM((6, 256, 128), F32),
            dma((2,)), dma((2,)), dma((2,)), dma((2,)), dma((2,)), dma((2,)), dma((6,)), dma((6,)),
        ],
        compiler_params=pltpu.CompilerParams(
            collective_id=0, has_side_effects=True, vmem_limit_bytes=60 * 1024 * 1024
        ),
    )(orbitals, potential.reshape(32, 128), kinetic, gradient, pair_coefs())
    return basis, blocks[None, None, None]


def solution(mesh):
    return jax.shard_map(
        on_device,
        mesh=mesh,
        in_specs=(P("gx", "gy", "gz", None), P("gx", "gy", "gz")),
        out_specs=(P("gx", "gy", "gz", None), P("gx", "gy", "gz", None, None, None)),
        check_vma=False,
    )
```

```python
import functools

import jax
import jax.numpy as jnp
import numpy as np
from jax import lax
from jax.experimental import pallas as pl
from jax.experimental.pallas import tpu as pltpu
from jax.sharding import PartitionSpec as P

BUF = 3
CELLS = 16
EXT = 22
ORB = 64
HALF = EXT // 2
OWN = CELLS // 2
PENALTY = 2.0
LOW_BOUND = -1.5
CUTOFF = 8.0
HIGH_BOUND = 16.0

YLO, YHI, ZLO, ZHI, CLO, CHI, ROWS = 256, 304, 352, 400, 448, 472, 496
INNER = 256
CROSS = 448
HALO, POT, PLANES = 8, 11, 12
CHUNKS = ((0, 128), (128, 128), (256, 136))
MESSAGE = 392
AXES = ("gx", "gy", "gz")
MESH = pl.DeviceIdType.MESH
F32 = jnp.float32
BF16 = jnp.bfloat16


def spectral_tables(points):
    indices = np.arange(points)
    offsets = indices[:, None] - indices[None, :]
    nyquist = points // 2
    deriv_one = np.zeros((points, points))
    deriv_two = np.zeros((points, points))
    for harmonic in range(1, nyquist):
        wavenum = 2.0 * np.pi * harmonic / points
        deriv_one = deriv_one - 2.0 * wavenum * np.sin(wavenum * offsets) / points
        deriv_two = deriv_two - 2.0 * wavenum * wavenum * np.cos(wavenum * offsets) / points
    deriv_two = deriv_two - np.pi * np.pi * np.cos(np.pi * offsets) / points
    return deriv_one, deriv_two


def row_cells():
    cells = [(-1, -1)] * ROWS
    for y in range(CELLS):
        for z in range(CELLS):
            cells[y * CELLS + z] = (BUF + y, BUF + z)
    for h in range(BUF):
        for k in range(CELLS):
            cells[YLO + h * CELLS + k] = (h, BUF + k)
            cells[YHI + h * CELLS + k] = (BUF + CELLS + h, BUF + k)
            cells[ZLO + h * CELLS + k] = (BUF + k, h)
            cells[ZHI + h * CELLS + k] = (BUF + k, BUF + CELLS + h)
        for k in range(2 * BUF):
            z = k if k < BUF else CELLS + k
            cells[CLO + h * 8 + k] = (h, z)
            cells[CHI + h * 8 + k] = (BUF + CELLS + h, z)
    return np.array(cells)


def split_host(matrix):
    full = jnp.asarray(matrix, F32)
    high = full.astype(BF16)
    low = (full - high.astype(F32)).astype(BF16)
    parts = [jnp.concatenate([m[:, k] for m in (high, low, high)], axis=1) for k in (slice(0, INNER), slice(INNER, None))]
    return jnp.concatenate(parts, axis=1)


def plane_matrices():
    deriv_one, deriv_two = spectral_tables(EXT)
    cells = row_cells()
    real = (cells[:, 0] >= 0).astype(np.float64)
    ys, zs = np.maximum(cells[:, 0], 0), np.maximum(cells[:, 1], 0)
    same_y = (ys[:, None] == ys[None, :]) * real[:, None] * real[None, :]
    same_z = (zs[:, None] == zs[None, :]) * real[:, None] * real[None, :]
    kinetic = -0.5 * (same_z * deriv_two[ys[:, None], ys[None, :]] + same_y * deriv_two[zs[:, None], zs[None, :]])
    grad_y = (same_z * deriv_one[ys[:, None], ys[None, :]])[:INNER, :CROSS]
    grad_z = (same_y * deriv_one[zs[:, None], zs[None, :]])[:INNER, :CROSS]
    return split_host(kinetic), split_host(np.concatenate([grad_y, grad_z], axis=0))


def pair_tables():
    deriv_one, deriv_two = spectral_tables(EXT)
    lanes = np.arange(128) < ORB

    def entry(table, factor, d):
        near, far = table[d % EXT, 0], table[(d + HALF) % EXT, 0]
        return factor * np.where(lanes, near + far, near - far)

    second, first = [], []
    two = lambda d: entry(deriv_two, -0.25, d)
    one = lambda d: entry(deriv_one, 0.5, d)
    keys_two, keys_one = {}, {}

    def put(keys, rows, key, value):
        keys[key] = len(rows)
        rows.append(value)

    for a in range(5):
        for b in range(a, 5):
            put(keys_two, second, ("e", a, b), 0.5 * (two(a - b) + two(10 - a - b)))
            put(keys_two, second, ("o", a, b), 0.5 * (two(a - b) - two(10 - a - b)))
    for d in range(6):
        put(keys_two, second, ("m", d), two(d))
    for a in range(5):
        for b in range(5):
            put(keys_one, first, ("q", a, b), 0.5 * (one(a - b) - one(a + b - 10)))
    for d in range(1, 6):
        put(keys_one, first, ("m", d), one(d))
    return np.array(second), keys_two, np.array(first), keys_one


SECOND, KEYS_TWO, FIRST, KEYS_ONE = pair_tables()


def cheb_constants():
    half_width = (HIGH_BOUND - CUTOFF) / 2.0
    center = (HIGH_BOUND + CUTOFF) / 2.0
    scale_now = half_width / (LOW_BOUND - center)
    scale_next = 1.0 / (2.0 / scale_now - scale_now)
    return center, scale_now / half_width, 2.0 * scale_next / half_width, scale_now * scale_next


def split(value):
    high = value.astype(BF16)
    return high, (value - high.astype(F32)).astype(BF16)


def stacked(value):
    high, low = split(value)
    return jnp.concatenate([high, high, low], axis=0)


def both_stacked(value):
    return jnp.concatenate([stacked(value[:INNER]), stacked(value[INNER:])], axis=0)


def swap(value):
    return pltpu.roll(value, ORB, 1)


def matmul(left, right):
    return jnp.dot(left, right, preferred_element_type=F32)


def gram(left, right):
    return lax.dot_general(left, right, (((0,), (0,)), ((), ())), preferred_element_type=F32)


def gram_split(left, right):
    (lh, ll), (rh, rl) = left, right
    return gram(lh, rh) + (gram(lh, rl) + gram(ll, rh))


def left_lanes(rows):
    return lax.broadcasted_iota(jnp.int32, (rows, 128), 1) < ORB


def kernel(
    x_hbm, pot_ref, kin_hbm, grad_hbm, two_ref, one_ref,
    basis_ref, blocks_ref,
    x_ref, kin_ref, grad_ref, spread_ref,
    xs, xr, flat, pot_s, cells, pots, work, filt, zs, cs, gx, gyz, faces, others,
    local, xsend, xrecv, ysend, yrecv, zsend, zrecv, csend, crecv, fsend, frecv,
):
    center, alpha, beta, gamma = cheb_constants()
    me = [lax.axis_index(a) for a in AXES]
    size = [lax.axis_size(a) for a in AXES]

    def beside(axis, step):
        return {AXES[axis]: lax.rem(me[axis] + step + size[axis], size[axis])}

    barrier = pltpu.get_barrier_semaphore()
    for axis in range(3):
        for step in (-1, 1):
            pl.semaphore_signal(barrier, inc=1, device_id=beside(axis, step), device_id_type=MESH)

    loads = [
        pltpu.make_async_copy(src, dst, local.at[k])
        for k, (src, dst) in enumerate(((x_hbm, x_ref), (kin_hbm, kin_ref), (grad_hbm, grad_ref)))
    ]
    for load in loads:
        load.start()

    def send(src, dst, ssem, rsem, axis, step):
        copy = pltpu.make_async_remote_copy(
            src_ref=src, dst_ref=dst, send_sem=ssem, recv_sem=rsem,
            device_id=beside(axis, step), device_id_type=MESH,
        )
        copy.start()
        return copy

    steps = (-1, 1)
    first = (0, CELLS - BUF)

    flat[...] = jnp.zeros_like(flat)
    flat[:, :CELLS] = pot_ref[...].reshape(INNER, CELLS)
    pot_s[...] = jnp.zeros_like(pot_s)
    xs[:, 384:392, :] = jnp.zeros((2, 8, 128), F32)
    for h in range(2):
        spread = flat[pl.ds(8 * h, CELLS, stride=CELLS), :]
        for m in range(1, 8):
            spread = spread + pltpu.roll(flat[pl.ds(8 * h + m, CELLS, stride=CELLS), :], CELLS * m, 1)
        pot_s[h, BUF : BUF + CELLS, :] = spread
        for side in range(2):
            xs[side, 384 + 4 * h : 387 + 4 * h, :] = pot_s[h, BUF + first[side] : 2 * BUF + first[side], :]
    loads[0].wait()
    for side in range(2):
        for j in range(BUF):
            xs[side, j * 128 : (j + 1) * 128, :] = jnp.concatenate(
                [x_ref[first[side] + j, :8].reshape(128, ORB), x_ref[first[side] + j, 8:].reshape(128, ORB)], axis=1
            )
    for i in range(OWN):
        cells[i, :INNER, :] = jnp.concatenate([x_ref[i].reshape(INNER, ORB), x_ref[OWN + i].reshape(INNER, ORB)], axis=1)

    def z_layers(p):
        for side in range(2):
            for h in range(BUF):
                zs[side, p, h * CELLS : (h + 1) * CELLS, :] = cells[p, pl.ds(first[side] + h, CELLS, stride=CELLS), :]

    def corners(p):
        for side in range(2):
            for h in range(BUF):
                cs[side, p, h * 8 : h * 8 + 6, :] = cells[p, pl.ds(ZLO + first[side] + h, 6, stride=CELLS), :]

    @pl.loop(0, OWN)
    def _(i):
        z_layers(i)

    cs[...] = jnp.zeros_like(cs)
    part = lax.broadcasted_iota(jnp.int32, (128, 128), 0)
    point = jnp.where(part < 96, lax.rem(part, 32), -1)
    halves = left_lanes(128)
    for p in range(POT):
        wanted = jnp.where(halves, BUF + p if p < OWN else p - OWN, HALF + p)
        spread_ref[:, p * 128 : (p + 1) * 128] = jnp.where(point == wanted, 1.0, 0.0).astype(BF16)
    pl.semaphore_wait(barrier, 6)

    def send_y(k, start, count):
        return [
            send(
                cells.at[pl.ds(start, count), pl.ds((0, 208)[side], 48), :],
                cells.at[pl.ds(start, count), pl.ds((YHI, YLO)[side], 48), :],
                ysend.at[side, k], yrecv.at[side, k], 1, steps[side],
            )
            for side in range(2)
        ]

    def send_z(k, start, count):
        return [
            send(
                zs.at[side, pl.ds(start, count)],
                cells.at[pl.ds(start, count), pl.ds((ZHI, ZLO)[side], 48), :],
                zsend.at[side, k], zrecv.at[side, k], 2, steps[side],
            )
            for side in range(2)
        ]

    def send_c(k, start, count):
        return [
            send(
                cs.at[side, pl.ds(start, count)],
                cells.at[pl.ds(start, count), pl.ds((CHI, CLO)[side], 24), :],
                csend.at[side, k], crecv.at[side, k], 1, steps[side],
            )
            for side in range(2)
        ]

    xcopies = []
    for j, (start, count) in enumerate(CHUNKS):
        xcopies.append([
            send(
                xs.at[side, pl.ds(start, count)], xr.at[side, pl.ds(start, count)],
                xsend.at[side, j], xrecv.at[side, j], 0, steps[side],
            )
            for side in range(2)
        ])
    ycopies = [send_y(0, 0, OWN)]
    zcopies = [send_z(0, 0, OWN)]
    ccopies = []

    def arrived(copies):
        for copy in copies:
            copy.wait_recv()

    def kinetic_part(planes, part, add):
        rows = slice(0, INNER) if part == 0 else slice(INNER, ROWS)
        cols = slice(0, 3 * INNER) if part == 0 else slice(3 * INNER, 3 * ROWS)

        def body(g):
            pair = jnp.concatenate([cells[2 * g, rows, :], cells[2 * g + 1, rows, :]], axis=1)
            done = matmul(kin_ref[:, cols], stacked(pair))
            work[2 * g] = work[2 * g] + done[:, :128] if add else done[:, :128]
            work[2 * g + 1] = work[2 * g + 1] + done[:, 128:] if add else done[:, 128:]

        pl.loop(planes[0], planes[1])(body)

    loads[1].wait()
    kinetic_part((0, OWN // 2), 0, False)
    keep = left_lanes(128)
    for j in range(BUF):
        arrived(xcopies[j])
        low = xr[1, j * 128 : (j + 1) * 128, :]
        high = xr[0, j * 128 : (j + 1) * 128, :]
        cells[HALO + j, 0:128, :] = jnp.where(keep, low, swap(high))
        cells[HALO + j, 128:256, :] = jnp.where(keep, swap(low), high)
        z_layers(HALO + j)
        if j == BUF - 1:
            for h in range(2):
                pot_s[h, 0:BUF, :] = xr[1, 384 + 4 * h : 387 + 4 * h, :]
                pot_s[h, BUF + CELLS : EXT, :] = xr[0, 384 + 4 * h : 387 + 4 * h, :]
                part = jnp.concatenate([pot_s[h], jnp.zeros((104, 128), F32)], axis=0)
                cells[POT, h * 128 : (h + 1) * 128, :] = part.T
            z_layers(POT)
        count = 2 if j == BUF - 1 else 1
        zcopies.append(send_z(1 + j, HALO + j, count))
        ycopies.append(send_y(1 + j, HALO + j, count))

    keep8 = left_lanes(8)
    sign = jnp.where(keep8, 1.0, -1.0).astype(F32)

    def load_pairs(planes):
        return [
            jnp.where(keep8, planes[HALO + a] if a < BUF else planes[a - BUF], planes[a] if a < OWN else planes[a])
            for a in range(HALF)
        ]

    def mix(pairs):
        return [swap(v) + sign * v for v in pairs]

    def unmix(total):
        return swap(total) + sign * total

    def fold(mixed):
        return (
            [mixed[b] + mixed[10 - b] for b in range(5)], [mixed[b] - mixed[10 - b] for b in range(5)], mixed[5],
        )

    def dot(coefs, values):
        total = coefs[0] * values[0]
        for c, v in zip(coefs[1:], values[1:]):
            total = total + c * v
        return total

    def table(ref, keys):
        return lambda *key: ref[keys[key] * 8 : keys[key] * 8 + 8, :]

    two, one = table(two_ref, KEYS_TWO), table(one_ref, KEYS_ONE)

    def second_along_x(pairs):
        even, odd, middle = fold(mix(pairs))
        out = [None] * HALF
        for a in range(5):
            near = dot([two("e", min(a, b), max(a, b)) for b in range(5)] + [two("m", 5 - a)], even + [middle])
            far = dot([two("o", min(a, b), max(a, b)) for b in range(5)], odd)
            out[a], out[10 - a] = unmix(near + far), unmix(near - far)
        out[5] = unmix(dot([two("m", 5 - b) for b in range(6)], even + [middle]))
        return out

    def first_along_x(pairs, wanted):
        even, odd, middle = fold(mix(pairs))
        out = [None] * HALF
        for a in range(5):
            if a not in wanted and 10 - a not in wanted:
                continue
            near = dot([one("q", b, a) for b in range(5)] + [one("m", 5 - a)], even + [middle])
            far = dot([one("q", a, b) for b in range(5)], odd)
            out[a] = unmix(far - near) if a in wanted else None
            out[10 - a] = unmix(far + near) if 10 - a in wanted else None
        if 5 in wanted:
            out[5] = unmix(dot([one("m", 5 - b) for b in range(5)], odd))
        return out

    def to_planes(pairs):
        own = [jnp.where(keep8, pairs[i + BUF], pairs[i]) for i in range(OWN)]
        return own + [jnp.where(keep8, pairs[j], pairs[OWN + j]) for j in range(BUF)]

    def tiles(start, stop, body):
        @pl.loop(start // 16, stop // 16)
        def _(r):
            for k in range(2):
                body(pl.ds(pl.multiple_of(r * 16 + k * 8, 8), 8))

    def spread_pot(rows):
        column = cells[POT, rows, :]
        high = column.astype(BF16).astype(F32)
        rest = column - high
        middle = rest.astype(BF16).astype(F32)
        parts = high + pltpu.roll(middle, 32, 1) + pltpu.roll(rest - middle, 64, 1)
        done = matmul(parts.astype(BF16), spread_ref[...])
        for p in range(POT):
            pots[p, rows, :] = done[:, p * 128 : (p + 1) * 128]

    def first_x(rows):
        planes = [cells[p, rows, :] for p in range(POT)]
        moved = to_planes(second_along_x(load_pairs(planes)))
        for p in range(POT):
            work[p, rows, :] = work[p, rows, :] + (moved[p] + (pots[p, rows, :] - center) * planes[p])

    kinetic_part((OWN // 2, PLANES // 2), 0, False)
    spread_pot(slice(0, INNER))
    tiles(0, INNER, first_x)

    arrived(zcopies[0])

    @pl.loop(0, OWN)
    def _(i):
        corners(i)

    ccopies.append(send_c(0, 0, OWN))
    for j in range(BUF):
        arrived(zcopies[1 + j])
        corners(HALO + j)
    corners(POT)
    ccopies.append(send_c(1, HALO, PLANES - HALO))
    for copies in ycopies:
        arrived(copies)
    spread_pot(slice(INNER, CROSS))
    tiles(INNER, CROSS, first_x)
    arrived(ccopies[0])
    kinetic_part((0, OWN // 2), 1, True)
    arrived(ccopies[1])
    spread_pot(slice(CROSS, ROWS))
    tiles(CROSS, ROWS, first_x)
    kinetic_part((OWN // 2, PLANES // 2), 1, True)

    def pair_of(ref, g, rows):
        return jnp.concatenate([ref[2 * g, :rows, :], ref[2 * g + 1, :rows, :]], axis=1)

    @pl.loop(0, PLANES // 2)
    def _(g):
        done = (alpha * beta) * matmul(kin_ref[:INNER, :], both_stacked(pair_of(work, g, ROWS)))
        filt[2 * g, :INNER, :] = done[:, :128]
        filt[2 * g + 1, :INNER, :] = done[:, 128:]

    def second_x(rows, count):
        planes = [work[p, rows, :] for p in range(POT)]
        moved = to_planes(second_along_x(load_pairs(planes)))
        values = []
        for p in range(count):
            applied = moved[p] + (pots[p, rows, :] - center) * planes[p]
            value = filt[p, rows, :] + ((alpha * beta) * applied - gamma * cells[p, rows, :])
            filt[p, rows, :] = value
            values.append(value)
        return values

    def inner_x(rows):
        values = second_x(rows, POT)
        slopes = first_along_x(load_pairs(values), (BUF, OWN - 1))
        low, high = slopes[BUF], slopes[OWN - 1]
        faces[0, rows, :] = jnp.where(keep8, values[0], swap(low))
        faces[1, rows, :] = jnp.where(keep8, swap(values[OWN - 1]), high)

    tiles(0, INNER, inner_x)
    fcopies = [None] * 6

    def send_faces(axis):
        fcopies[2 * axis] = send(faces.at[2 * axis], others.at[2 * axis + 1], fsend.at[2 * axis], frecv.at[2 * axis + 1], axis, -1)
        fcopies[2 * axis + 1] = send(faces.at[2 * axis + 1], others.at[2 * axis], fsend.at[2 * axis + 1], frecv.at[2 * axis], axis, 1)

    send_faces(0)

    @pl.loop(0, OWN // 2)
    def _(g):
        done = (alpha * beta) * matmul(kin_ref[INNER:CROSS, :], both_stacked(pair_of(work, g, ROWS)))
        filt[2 * g, INNER:CROSS, :] = done[:, :128]
        filt[2 * g + 1, INNER:CROSS, :] = done[:, 128:]

    def outer_x(rows):
        second_x(rows, OWN)

    tiles(INNER, CROSS, outer_x)

    loads[2].wait()

    @pl.loop(0, OWN // 2)
    def _(g):
        done = matmul(grad_ref[...], both_stacked(pair_of(filt, g, CROSS)))
        gyz[2 * g] = done[:, :128]
        gyz[2 * g + 1] = done[:, 128:]

    keep16 = left_lanes(16)
    for i in range(OWN):
        for side, layer in ((0, 0), (1, CELLS - 1)):
            for f, value, deriv in (
                (2 + side, filt[i, layer * 16 : layer * 16 + 16, :], gyz[i, layer * 16 : layer * 16 + 16, :]),
                (4 + side, filt[i, pl.ds(layer, 16, stride=16), :], gyz[i, pl.ds(INNER + layer, 16, stride=16), :]),
            ):
                faces[f, i * 16 : i * 16 + 16, :] = jnp.where(keep16, value, swap(deriv))
                faces[f, 128 + i * 16 : 144 + i * 16, :] = jnp.where(keep16, swap(value), deriv)
    send_faces(1)
    send_faces(2)

    def full_gx(rows):
        planes = [filt[p, rows, :] for p in range(POT)]
        moved = first_along_x(load_pairs(planes), range(HALF))
        for i in range(OWN):
            gx[i, rows, :] = jnp.where(keep8, moved[i + BUF], moved[i])

    tiles(0, INNER, full_gx)
    basis_ref[...] = filt[:OWN, :INNER, :]

    def volume(i, total):
        value = filt[i, :INNER, :]
        left, left_low = split(value)
        right, right_low = split(2.0 * pots[i, :INNER, :] * value)
        slopes = [split(part) for part in (gx[i], gyz[i, :INNER, :], gyz[i, INNER:, :])]
        lefts = [left] + [high for high, _ in slopes]
        rights = [right] + [high for high, _ in slopes] + [right_low] + [2.0 * low for _, low in slopes] + [right]
        return total + gram(jnp.concatenate(lefts + lefts + [left_low], axis=0), jnp.concatenate(rights, axis=0))

    total = lax.fori_loop(0, OWN, volume, jnp.zeros((128, 128), F32))
    total = 0.25 * (total + total.T)
    diagonal = total[:ORB, :ORB] + total[ORB:, ORB:]
    for f in range(6):
        s = -1.0 if f % 2 == 0 else 1.0
        pair = split(faces[f])
        own = gram_split(pair, pair)
        diagonal = diagonal - (0.25 * s) * (own[:ORB, ORB:] + own[ORB:, :ORB]) + (0.5 * PENALTY) * own[:ORB, :ORB]
    blocks_ref[0] = diagonal
    for f in (2, 3, 4, 5, 0, 1):
        fcopies[f ^ 1].wait_recv()
        s = -1.0 if f % 2 == 0 else 1.0
        both = gram_split(split(faces[f]), split(others[f]))
        blocks_ref[1 + f] = (0.25 * s) * (both[ORB:, :ORB] - both[:ORB, ORB:]) - (0.5 * PENALTY) * both[:ORB, :ORB]
    for copies in xcopies + ycopies + zcopies + ccopies + [fcopies]:
        for copy in copies:
            copy.wait_send()


def unpack_kernel(packed_ref, blocks_in, basis_ref, blocks_ref):
    blocks_ref[...] = blocks_in[...]
    for i in range(OWN):
        value = packed_ref[i]
        basis_ref[i] = value[:, :ORB].reshape(CELLS, CELLS, ORB)
        basis_ref[OWN + i] = swap(value)[:, :ORB].reshape(CELLS, CELLS, ORB)


def on_device(orbitals, potential):
    kinetic, gradient = plane_matrices()
    vmem = pl.BlockSpec(memory_space=pltpu.VMEM)
    hbm = pl.BlockSpec(memory_space=pl.ANY)
    dma = pltpu.SemaphoreType.DMA
    blocks_shape = jax.ShapeDtypeStruct((7, ORB, ORB), F32)
    tables = [jnp.asarray(np.repeat(t, 8, axis=0), F32) for t in (SECOND, FIRST)]
    packed, blocks = pl.pallas_call(
        kernel,
        out_shape=(jax.ShapeDtypeStruct((OWN, INNER, 128), F32), blocks_shape),
        in_specs=[hbm, vmem, hbm, hbm, vmem, vmem],
        out_specs=(vmem, vmem),
        scratch_shapes=[
            pltpu.VMEM((CELLS, CELLS, CELLS, ORB), F32),
            pltpu.VMEM(kinetic.shape, BF16),
            pltpu.VMEM(gradient.shape, BF16),
            pltpu.VMEM((128, POT * 128), BF16),
            pltpu.VMEM((2, MESSAGE, 128), F32),
            pltpu.VMEM((2, MESSAGE, 128), F32),
            pltpu.VMEM((INNER, 128), F32),
            pltpu.VMEM((2, 24, 128), F32),
            pltpu.VMEM((PLANES, ROWS, 128), F32),
            pltpu.VMEM((POT, ROWS, 128), F32),
            pltpu.VMEM((PLANES, ROWS, 128), F32),
            pltpu.VMEM((PLANES, CROSS, 128), F32),
            pltpu.VMEM((2, PLANES, 48, 128), F32),
            pltpu.VMEM((2, PLANES, 24, 128), F32),
            pltpu.VMEM((OWN, INNER, 128), F32),
            pltpu.VMEM((OWN, 2 * INNER, 128), F32),
            pltpu.VMEM((6, INNER, 128), F32),
            pltpu.VMEM((6, INNER, 128), F32),
            dma((3,)),
            dma((2, 3)), dma((2, 3)), dma((2, 4)), dma((2, 4)), dma((2, 4)), dma((2, 4)),
            dma((2, 2)), dma((2, 2)), dma((6,)), dma((6,)),
        ],
        compiler_params=pltpu.CompilerParams(
            collective_id=0, has_side_effects=True, vmem_limit_bytes=60 * 1024 * 1024
        ),
    )(orbitals, potential, kinetic, gradient, *tables)
    basis, blocks = pl.pallas_call(
        unpack_kernel,
        out_shape=(jax.ShapeDtypeStruct((CELLS, CELLS, CELLS, ORB), F32), blocks_shape),
        in_specs=[vmem, vmem],
        out_specs=(vmem, vmem),
    )(packed, blocks)
    return basis, blocks[None, None, None]


def solution(mesh):
    return jax.shard_map(
        on_device,
        mesh=mesh,
        in_specs=(P("gx", "gy", "gz", None), P("gx", "gy", "gz")),
        out_specs=(P("gx", "gy", "gz", None), P("gx", "gy", "gz", None, None, None)),
        check_vma=False,
    )
```

```python
import functools

import jax
import jax.numpy as jnp
import numpy as np
from jax import lax
from jax.experimental import pallas as pl
from jax.experimental.pallas import tpu as pltpu
from jax.sharding import PartitionSpec as P

BUF = 3
CELLS = 16
EXT = 22
ORB = 64
HALF = EXT // 2
OWN = CELLS // 2
PENALTY = 2.0
LOW_BOUND = -1.5
CUTOFF = 8.0
HIGH_BOUND = 16.0

YLO, YHI, ZLO, ZHI, CLO, CHI, ROWS = 256, 304, 352, 400, 448, 472, 496
INNER = 256
CROSS = 448
HALO, POT, PLANES = 8, 11, 12
CHUNKS = ((0, 128), (128, 128), (256, 136))
MESSAGE = 392
AXES = ("gx", "gy", "gz")
MESH = pl.DeviceIdType.MESH
F32 = jnp.float32
BF16 = jnp.bfloat16


def spectral_tables(points):
    indices = np.arange(points)
    offsets = indices[:, None] - indices[None, :]
    nyquist = points // 2
    deriv_one = np.zeros((points, points))
    deriv_two = np.zeros((points, points))
    for harmonic in range(1, nyquist):
        wavenum = 2.0 * np.pi * harmonic / points
        deriv_one = deriv_one - 2.0 * wavenum * np.sin(wavenum * offsets) / points
        deriv_two = deriv_two - 2.0 * wavenum * wavenum * np.cos(wavenum * offsets) / points
    deriv_two = deriv_two - np.pi * np.pi * np.cos(np.pi * offsets) / points
    return deriv_one, deriv_two


def row_cells():
    cells = [(-1, -1)] * ROWS
    for y in range(CELLS):
        for z in range(CELLS):
            cells[y * CELLS + z] = (BUF + y, BUF + z)
    for h in range(BUF):
        for k in range(CELLS):
            cells[YLO + h * CELLS + k] = (h, BUF + k)
            cells[YHI + h * CELLS + k] = (BUF + CELLS + h, BUF + k)
            cells[ZLO + h * CELLS + k] = (BUF + k, h)
            cells[ZHI + h * CELLS + k] = (BUF + k, BUF + CELLS + h)
        for k in range(2 * BUF):
            z = k if k < BUF else CELLS + k
            cells[CLO + h * 8 + k] = (h, z)
            cells[CHI + h * 8 + k] = (BUF + CELLS + h, z)
    return np.array(cells)


def split_host(matrix):
    full = jnp.asarray(matrix, F32)
    high = full.astype(BF16)
    low = (full - high.astype(F32)).astype(BF16)
    parts = [jnp.concatenate([m[:, k] for m in (high, low, high)], axis=1) for k in (slice(0, INNER), slice(INNER, None))]
    return jnp.concatenate(parts, axis=1)


def plane_matrices():
    deriv_one, deriv_two = spectral_tables(EXT)
    cells = row_cells()
    real = (cells[:, 0] >= 0).astype(np.float64)
    ys, zs = np.maximum(cells[:, 0], 0), np.maximum(cells[:, 1], 0)
    same_y = (ys[:, None] == ys[None, :]) * real[:, None] * real[None, :]
    same_z = (zs[:, None] == zs[None, :]) * real[:, None] * real[None, :]
    kinetic = -0.5 * (same_z * deriv_two[ys[:, None], ys[None, :]] + same_y * deriv_two[zs[:, None], zs[None, :]])
    grad_y = (same_z * deriv_one[ys[:, None], ys[None, :]])[:INNER, :CROSS]
    grad_z = (same_y * deriv_one[zs[:, None], zs[None, :]])[:INNER, :CROSS]
    return split_host(kinetic), split_host(np.concatenate([grad_y, grad_z], axis=0))


def pair_tables():
    deriv_one, deriv_two = spectral_tables(EXT)
    lanes = np.arange(128) < ORB

    def entry(table, factor, d):
        near, far = table[d % EXT, 0], table[(d + HALF) % EXT, 0]
        return factor * np.where(lanes, near + far, near - far)

    second, first = [], []
    two = lambda d: entry(deriv_two, -0.25, d)
    one = lambda d: entry(deriv_one, 0.5, d)
    keys_two, keys_one = {}, {}

    def put(keys, rows, key, value):
        keys[key] = len(rows)
        rows.append(value)

    for a in range(5):
        for b in range(a, 5):
            put(keys_two, second, ("e", a, b), 0.5 * (two(a - b) + two(10 - a - b)))
            put(keys_two, second, ("o", a, b), 0.5 * (two(a - b) - two(10 - a - b)))
    for d in range(6):
        put(keys_two, second, ("m", d), two(d))
    for a in range(5):
        for b in range(5):
            put(keys_one, first, ("q", a, b), 0.5 * (one(a - b) - one(a + b - 10)))
    for d in range(1, 6):
        put(keys_one, first, ("m", d), one(d))
    return np.array(second), keys_two, np.array(first), keys_one


SECOND, KEYS_TWO, FIRST, KEYS_ONE = pair_tables()


def cheb_constants():
    half_width = (HIGH_BOUND - CUTOFF) / 2.0
    center = (HIGH_BOUND + CUTOFF) / 2.0
    scale_now = half_width / (LOW_BOUND - center)
    scale_next = 1.0 / (2.0 / scale_now - scale_now)
    return center, scale_now / half_width, 2.0 * scale_next / half_width, scale_now * scale_next


def split(value):
    high = value.astype(BF16)
    return high, (value - high.astype(F32)).astype(BF16)


def stacked(value):
    high, low = split(value)
    return jnp.concatenate([high, high, low], axis=0)


def both_stacked(value):
    return jnp.concatenate([stacked(value[:INNER]), stacked(value[INNER:])], axis=0)


def swap(value):
    return pltpu.roll(value, ORB, 1)


def matmul(left, right):
    return jnp.dot(left, right, preferred_element_type=F32)


def gram(left, right):
    return lax.dot_general(left, right, (((0,), (0,)), ((), ())), preferred_element_type=F32)


def gram_split(left, right):
    (lh, ll), (rh, rl) = left, right
    return gram(lh, rh) + (gram(lh, rl) + gram(ll, rh))


def left_lanes(rows):
    return lax.broadcasted_iota(jnp.int32, (rows, 128), 1) < ORB


def kernel(
    x_hbm, pot_ref, kin_hbm, grad_hbm, two_ref, one_ref,
    basis_ref, blocks_ref,
    x_ref, kin_ref, grad_ref, spread_ref, done_ref, rest_ref, mids, backs, bundle,
    xs, xr, flat, pot_s, cells, pots, work, filt, zs, cs, gx, gyz, faces, others,
    local, xsend, xrecv, ysend, yrecv, zsend, zrecv, csend, crecv, fsend, frecv, msend, mrecv,
):
    center, alpha, beta, gamma = cheb_constants()
    me = [lax.axis_index(a) for a in AXES]
    size = [lax.axis_size(a) for a in AXES]

    def beside(axis, step):
        return {AXES[axis]: lax.rem(me[axis] + step + size[axis], size[axis])}

    ring = size[2]
    reach = ring // 4

    def along_y(gx, gz, step):
        position = lax.rem(lax.rem(gx, 2) * (ring // 2) + gz // 2 + step + ring, ring)
        return (
            gx // 2 * 2 + position // (ring // 2),
            lax.rem(position, ring // 2) * 2 + lax.rem(gz, 2),
        )

    def device(gx, gz):
        return {AXES[0]: gx, AXES[2]: gz}

    below = lax.rem(me[0] + size[0] - 1, size[0])
    upper_mid = device(*along_y(me[0], me[2], reach))
    lower_mid = device(*along_y(below, me[2], reach))
    served_gx, served_gz = along_y(me[0], me[2], -reach)
    served = device(served_gx, served_gz)
    served_next = device(lax.rem(served_gx + 1, size[0]), served_gz)

    barrier = pltpu.get_barrier_semaphore()
    partners = [beside(axis, step) for axis in range(3) for step in (-1, 1)]
    partners += [upper_mid, lower_mid, served, served_next]
    for partner in partners:
        pl.semaphore_signal(barrier, inc=1, device_id=partner, device_id_type=MESH)

    loads = [
        pltpu.make_async_copy(src, dst, local.at[k])
        for k, (src, dst) in enumerate(((x_hbm, x_ref), (kin_hbm, kin_ref), (grad_hbm, grad_ref)))
    ]
    for load in loads:
        load.start()

    def send_to(src, dst, ssem, rsem, target):
        copy = pltpu.make_async_remote_copy(
            src_ref=src, dst_ref=dst, send_sem=ssem, recv_sem=rsem, device_id=target, device_id_type=MESH,
        )
        copy.start()
        return copy

    def send(src, dst, ssem, rsem, axis, step):
        return send_to(src, dst, ssem, rsem, beside(axis, step))

    steps = (-1, 1)
    first = (0, CELLS - BUF)

    flat[...] = jnp.zeros_like(flat)
    flat[:, :CELLS] = pot_ref[...].reshape(INNER, CELLS)
    pot_s[...] = jnp.zeros_like(pot_s)
    xs[:, 384:392, :] = jnp.zeros((2, 8, 128), F32)
    for h in range(2):
        spread = flat[pl.ds(8 * h, CELLS, stride=CELLS), :]
        for m in range(1, 8):
            spread = spread + pltpu.roll(flat[pl.ds(8 * h + m, CELLS, stride=CELLS), :], CELLS * m, 1)
        pot_s[h, BUF : BUF + CELLS, :] = spread
        for side in range(2):
            xs[side, 384 + 4 * h : 387 + 4 * h, :] = pot_s[h, BUF + first[side] : 2 * BUF + first[side], :]
    loads[0].wait()
    for side in range(2):
        for j in range(BUF):
            xs[side, j * 128 : (j + 1) * 128, :] = jnp.concatenate(
                [x_ref[first[side] + j, :8].reshape(128, ORB), x_ref[first[side] + j, 8:].reshape(128, ORB)], axis=1
            )
    for i in range(OWN):
        cells[i, :INNER, :] = jnp.concatenate([x_ref[i].reshape(INNER, ORB), x_ref[OWN + i].reshape(INNER, ORB)], axis=1)

    def z_layers(p):
        for side in range(2):
            for h in range(BUF):
                zs[side, p, h * CELLS : (h + 1) * CELLS, :] = cells[p, pl.ds(first[side] + h, CELLS, stride=CELLS), :]

    def corners(p):
        for side in range(2):
            for h in range(BUF):
                cs[side, p, h * 8 : h * 8 + 6, :] = cells[p, pl.ds(ZLO + first[side] + h, 6, stride=CELLS), :]

    @pl.loop(0, OWN)
    def _(i):
        z_layers(i)

    cs[...] = jnp.zeros_like(cs)
    part = lax.broadcasted_iota(jnp.int32, (128, 128), 0)
    point = jnp.where(part < 96, lax.rem(part, 32), -1)
    halves = left_lanes(128)
    for p in range(POT):
        wanted = jnp.where(halves, BUF + p if p < OWN else p - OWN, HALF + p)
        spread_ref[:, p * 128 : (p + 1) * 128] = jnp.where(point == wanted, 1.0, 0.0).astype(BF16)
    pl.semaphore_wait(barrier, 10)

    def send_y(k, start, count):
        return [
            send(
                cells.at[pl.ds(start, count), pl.ds((0, 208)[side], 48), :],
                cells.at[pl.ds(start, count), pl.ds((YHI, YLO)[side], 48), :],
                ysend.at[side, k], yrecv.at[side, k], 1, steps[side],
            )
            for side in range(2)
        ]

    def send_z(k, start, count):
        return [
            send(
                zs.at[side, pl.ds(start, count)],
                cells.at[pl.ds(start, count), pl.ds((ZHI, ZLO)[side], 48), :],
                zsend.at[side, k], zrecv.at[side, k], 2, steps[side],
            )
            for side in range(2)
        ]

    def send_c(k, start, count):
        return [
            send(
                cs.at[side, pl.ds(start, count)],
                cells.at[pl.ds(start, count), pl.ds((CHI, CLO)[side], 24), :],
                csend.at[side, k], crecv.at[side, k], 1, steps[side],
            )
            for side in range(2)
        ]

    xcopies = []
    for j, (start, count) in enumerate(CHUNKS):
        xcopies.append([
            send(
                xs.at[side, pl.ds(start, count)], xr.at[side, pl.ds(start, count)],
                xsend.at[side, j], xrecv.at[side, j], 0, steps[side],
            )
            for side in range(2)
        ])
    ycopies = [send_y(0, 0, OWN)]
    zcopies = [send_z(0, 0, OWN)]
    ccopies = []

    def arrived(copies):
        for copy in copies:
            copy.wait_recv()

    def kinetic_part(planes, part, add):
        rows = slice(0, INNER) if part == 0 else slice(INNER, ROWS)
        cols = slice(0, 3 * INNER) if part == 0 else slice(3 * INNER, 3 * ROWS)

        def body(g):
            pair = jnp.concatenate([cells[2 * g, rows, :], cells[2 * g + 1, rows, :]], axis=1)
            done = matmul(kin_ref[:, cols], stacked(pair))
            work[2 * g] = work[2 * g] + done[:, :128] if add else done[:, :128]
            work[2 * g + 1] = work[2 * g + 1] + done[:, 128:] if add else done[:, 128:]

        pl.loop(planes[0], planes[1])(body)

    loads[1].wait()
    kinetic_part((0, OWN // 2), 0, False)
    keep = left_lanes(128)
    for j in range(BUF):
        arrived(xcopies[j])
        low = xr[1, j * 128 : (j + 1) * 128, :]
        high = xr[0, j * 128 : (j + 1) * 128, :]
        cells[HALO + j, 0:128, :] = jnp.where(keep, low, swap(high))
        cells[HALO + j, 128:256, :] = jnp.where(keep, swap(low), high)
        z_layers(HALO + j)
        if j == BUF - 1:
            for h in range(2):
                pot_s[h, 0:BUF, :] = xr[1, 384 + 4 * h : 387 + 4 * h, :]
                pot_s[h, BUF + CELLS : EXT, :] = xr[0, 384 + 4 * h : 387 + 4 * h, :]
                part = jnp.concatenate([pot_s[h], jnp.zeros((104, 128), F32)], axis=0)
                cells[POT, h * 128 : (h + 1) * 128, :] = part.T
            z_layers(POT)
        count = 2 if j == BUF - 1 else 1
        zcopies.append(send_z(1 + j, HALO + j, count))
        ycopies.append(send_y(1 + j, HALO + j, count))

    keep8 = left_lanes(8)
    sign = jnp.where(keep8, 1.0, -1.0).astype(F32)

    def load_pairs(planes):
        return [
            jnp.where(keep8, planes[HALO + a] if a < BUF else planes[a - BUF], planes[a] if a < OWN else planes[a])
            for a in range(HALF)
        ]

    def mix(pairs):
        return [swap(v) + sign * v for v in pairs]

    def unmix(total):
        return swap(total) + sign * total

    def fold(mixed):
        return (
            [mixed[b] + mixed[10 - b] for b in range(5)], [mixed[b] - mixed[10 - b] for b in range(5)], mixed[5],
        )

    def dot(coefs, values):
        total = coefs[0] * values[0]
        for c, v in zip(coefs[1:], values[1:]):
            total = total + c * v
        return total

    def table(ref, keys):
        return lambda *key: ref[keys[key] * 8 : keys[key] * 8 + 8, :]

    two, one = table(two_ref, KEYS_TWO), table(one_ref, KEYS_ONE)

    def second_along_x(pairs):
        even, odd, middle = fold(mix(pairs))
        out = [None] * HALF
        for a in range(5):
            near = dot([two("e", min(a, b), max(a, b)) for b in range(5)] + [two("m", 5 - a)], even + [middle])
            far = dot([two("o", min(a, b), max(a, b)) for b in range(5)], odd)
            out[a], out[10 - a] = unmix(near + far), unmix(near - far)
        out[5] = unmix(dot([two("m", 5 - b) for b in range(6)], even + [middle]))
        return out

    def first_along_x(pairs, wanted):
        even, odd, middle = fold(mix(pairs))
        out = [None] * HALF
        for a in range(5):
            if a not in wanted and 10 - a not in wanted:
                continue
            near = dot([one("q", b, a) for b in range(5)] + [one("m", 5 - a)], even + [middle])
            far = dot([one("q", a, b) for b in range(5)], odd)
            out[a] = unmix(far - near) if a in wanted else None
            out[10 - a] = unmix(far + near) if 10 - a in wanted else None
        if 5 in wanted:
            out[5] = unmix(dot([one("m", 5 - b) for b in range(5)], odd))
        return out

    def to_planes(pairs):
        own = [jnp.where(keep8, pairs[i + BUF], pairs[i]) for i in range(OWN)]
        return own + [jnp.where(keep8, pairs[j], pairs[OWN + j]) for j in range(BUF)]

    def tile(r):
        return pl.ds(pl.multiple_of(r * 8, 8), 8)

    def tiles(start, stop, body):
        @pl.loop(start // 16, stop // 16)
        def _(r):
            for k in range(2):
                body(tile(2 * r + k))

    def spread_pot(rows):
        column = cells[POT, rows, :]
        high = column.astype(BF16).astype(F32)
        rest = column - high
        middle = rest.astype(BF16).astype(F32)
        parts = high + pltpu.roll(middle, 32, 1) + pltpu.roll(rest - middle, 64, 1)
        done = matmul(parts.astype(BF16), spread_ref[...])
        for p in range(POT):
            pots[p, rows, :] = done[:, p * 128 : (p + 1) * 128]

    def first_x(rows):
        planes = [cells[p, rows, :] for p in range(POT)]
        moved = to_planes(second_along_x(load_pairs(planes)))
        for p in range(POT):
            work[p, rows, :] = work[p, rows, :] + (moved[p] + (pots[p, rows, :] - center) * planes[p])

    kinetic_part((OWN // 2, PLANES // 2), 0, False)
    spread_pot(slice(0, INNER))
    tiles(0, INNER, first_x)

    arrived(zcopies[0])

    @pl.loop(0, OWN)
    def _(i):
        corners(i)

    ccopies.append(send_c(0, 0, OWN))
    for j in range(BUF):
        arrived(zcopies[1 + j])
        corners(HALO + j)
    corners(POT)
    ccopies.append(send_c(1, HALO, PLANES - HALO))
    for copies in ycopies:
        arrived(copies)
    spread_pot(slice(INNER, CROSS))
    tiles(INNER, CROSS, first_x)
    arrived(ccopies[0])
    kinetic_part((0, OWN // 2), 1, True)
    arrived(ccopies[1])
    spread_pot(slice(CROSS, ROWS))
    tiles(CROSS, ROWS, first_x)
    kinetic_part((OWN // 2, PLANES // 2), 1, True)

    def pair_of(ref, g, rows):
        return jnp.concatenate([ref[2 * g, :rows, :], ref[2 * g + 1, :rows, :]], axis=1)

    def second_x(rows):
        planes = [work[p, rows, :] for p in range(POT)]
        moved = to_planes(second_along_x(load_pairs(planes)))
        return [
            (alpha * beta) * (moved[p] + (pots[p, rows, :] - center) * planes[p]) - gamma * cells[p, rows, :]
            for p in range(POT)
        ]

    @pl.loop(0, PLANES // 2)
    def _(g):
        done = (alpha * beta) * matmul(kin_ref[:INNER, :], both_stacked(pair_of(work, g, ROWS)))
        done_ref[2 * g] = done[:, :128]
        done_ref[2 * g + 1] = done[:, 128:]
        for k in range(6):
            rows = tile(6 * g + k)
            for p, value in enumerate(second_x(rows)):
                filt[p, rows, :] = value

    @pl.loop(0, OWN // 2)
    def _(g):
        done = (alpha * beta) * matmul(kin_ref[INNER:CROSS, :], both_stacked(pair_of(work, g, ROWS)))
        rest_ref[2 * g] = done[:, :128]
        rest_ref[2 * g + 1] = done[:, 128:]
        for k in range(8):
            rows = tile(8 * g + k)
            values = [filt[p, rows, :] + done_ref[p, rows, :] for p in range(POT)]
            slopes = first_along_x(load_pairs(values), (BUF, OWN - 1))
            for p in range(POT):
                filt[p, rows, :] = values[p]
            faces[0, rows, :] = jnp.where(keep8, values[0], swap(slopes[BUF]))
            faces[1, rows, :] = jnp.where(keep8, swap(values[OWN - 1]), slopes[OWN - 1])

    fcopies = [
        send_to(faces.at[0], mids.at[1], fsend.at[0], frecv.at[0], lower_mid),
        send_to(faces.at[1], mids.at[0], fsend.at[1], frecv.at[1], upper_mid),
    ]
    result = pltpu.make_async_copy(filt.at[pl.ds(0, OWN), pl.ds(0, INNER), :], basis_ref, local.at[3])
    result.start()

    for i in range(OWN):
        filt[i, INNER : INNER + 32, :] = filt[i, INNER : INNER + 32, :] + rest_ref[i, :32, :]

    @pl.loop(18, CROSS // 16)
    def _(r):
        for k in range(2):
            rows = tile(2 * r + k)
            shifted = tile(2 * r + k - INNER // 8)
            values = second_x(rows)
            for i in range(OWN):
                filt[i, rows, :] = values[i] + rest_ref[i, shifted, :]

    loads[2].wait()

    @pl.loop(0, OWN // 2)
    def _(g):
        done = matmul(grad_ref[...], both_stacked(pair_of(filt, g, CROSS)))
        gyz[2 * g] = done[:, :128]
        gyz[2 * g + 1] = done[:, 128:]
        for k in range(8):
            rows = tile(8 * g + k)
            moved = first_along_x(load_pairs([filt[p, rows, :] for p in range(POT)]), range(HALF))
            for i in range(OWN):
                gx[i, rows, :] = jnp.where(keep8, moved[i + BUF], moved[i])

    keep16 = left_lanes(16)
    for i in range(OWN):
        for side, layer in ((0, 0), (1, CELLS - 1)):
            for f, value, deriv in (
                (2 + side, filt[i, layer * 16 : layer * 16 + 16, :], gyz[i, layer * 16 : layer * 16 + 16, :]),
                (4 + side, filt[i, pl.ds(layer, 16, stride=16), :], gyz[i, pl.ds(INNER + layer, 16, stride=16), :]),
            ):
                faces[f, i * 16 : i * 16 + 16, :] = jnp.where(keep16, value, swap(deriv))
                faces[f, 128 + i * 16 : 144 + i * 16, :] = jnp.where(keep16, swap(value), deriv)
    for axis in (1, 2):
        for side in range(2):
            f = 2 * axis + side
            fcopies.append(send(faces.at[f], others.at[f ^ 1], fsend.at[f], frecv.at[f ^ 1], axis, steps[side]))

    def volume(i, total):
        value = filt[i, :INNER, :]
        left, left_low = split(value)
        right, right_low = split(2.0 * pots[i, :INNER, :] * value)
        slopes = [split(part) for part in (gx[i], gyz[i, :INNER, :], gyz[i, INNER:, :])]
        lefts = jnp.concatenate([left] + [high for high, _ in slopes], axis=0)
        rights = jnp.concatenate([right] + [high for high, _ in slopes], axis=0)
        lows = jnp.concatenate([right_low] + [2.0 * low for _, low in slopes], axis=0)
        many = gram(lefts, jnp.concatenate([rights, lows], axis=1))
        return total + (many[:, :128] + many[:, 128:]) + gram(left_low, right)

    keep256 = left_lanes(256)

    def product(face, right):
        high, low = split(face)
        right_high, right_low = split(right)
        width = right.shape[1]
        many = gram(high, jnp.concatenate([right_high, right_low], axis=1))
        return many[:, :width] + many[:, width:] + gram(low, right_high)

    def coupling_right(other, s):
        flipped = swap(other)
        return jnp.where(keep256, (-0.5 * PENALTY) * other - (0.25 * s) * flipped, (0.25 * s) * flipped)

    def own_right(face, s):
        return jnp.where(keep256, (0.25 * PENALTY) * face - (0.25 * s) * swap(face), 0.0)

    total = lax.fori_loop(0, 5, volume, jnp.zeros((128, 128), F32))

    fcopies[0].wait_recv()
    fcopies[1].wait_recv()
    both = product(mids[0], coupling_right(mids[1], 1.0))
    block = both[:ORB, :ORB] + both[ORB:, ORB:]
    for side, value in ((0, block), (1, block.T)):
        bundle[side] = jnp.concatenate([value[: ORB // 2], value[ORB // 2 :]], axis=1)
    mcopies = [
        send_to(bundle.at[0], backs.at[1], msend.at[0], mrecv.at[1], served),
        send_to(bundle.at[1], backs.at[0], msend.at[1], mrecv.at[0], served_next),
    ]

    total = lax.fori_loop(5, OWN, volume, total)
    total = 0.25 * (total + total.T)
    diagonal = total[:ORB, :ORB] + total[ORB:, ORB:]
    halves = jnp.zeros((128, 128), F32)
    for f in range(2):
        halves = halves + product(faces[f], own_right(faces[f], 2.0 * f - 1.0))
    for f in range(2, 6):
        fcopies[f].wait_recv()

    def face_terms(f, halves):
        s = 2.0 * lax.rem(f, 2).astype(F32) - 1.0
        right = jnp.concatenate([coupling_right(others[f], s), own_right(faces[f], s)], axis=1)
        both = product(faces[f], right)
        blocks_ref[1 + f] = both[:ORB, :ORB] + both[ORB:, ORB:128]
        return halves + both[:, 128:]

    halves = lax.fori_loop(2, 6, face_terms, halves)[:ORB, :ORB]
    blocks_ref[0] = diagonal + (halves + halves.T)
    for side in range(2):
        mcopies[1 - side].wait_recv()
        got = backs[side]
        blocks_ref[1 + side, : ORB // 2, :] = got[:, :ORB]
        blocks_ref[1 + side, ORB // 2 :, :] = swap(got)[:, :ORB]
    result.wait()
    for copies in xcopies + ycopies + zcopies + ccopies + [fcopies, mcopies]:
        for copy in copies:
            copy.wait_send()


def on_device(orbitals, potential):
    kinetic, gradient = plane_matrices()
    vmem = pl.BlockSpec(memory_space=pltpu.VMEM)
    hbm = pl.BlockSpec(memory_space=pl.ANY)
    dma = pltpu.SemaphoreType.DMA
    blocks_shape = jax.ShapeDtypeStruct((7, ORB, ORB), F32)
    tables = [jnp.asarray(np.repeat(t, 8, axis=0), F32) for t in (SECOND, FIRST)]
    packed, blocks = pl.pallas_call(
        kernel,
        out_shape=(jax.ShapeDtypeStruct((OWN, INNER, 128), F32), blocks_shape),
        in_specs=[hbm, vmem, hbm, hbm, vmem, vmem],
        out_specs=(hbm, vmem),
        scratch_shapes=[
            pltpu.VMEM((CELLS, CELLS, CELLS, ORB), F32),
            pltpu.VMEM(kinetic.shape, BF16),
            pltpu.VMEM(gradient.shape, BF16),
            pltpu.VMEM((128, POT * 128), BF16),
            pltpu.VMEM((PLANES, INNER, 128), F32),
            pltpu.VMEM((OWN, CROSS - INNER, 128), F32),
            pltpu.VMEM((2, INNER, 128), F32),
            pltpu.VMEM((2, ORB // 2, 128), F32),
            pltpu.VMEM((2, ORB // 2, 128), F32),
            pltpu.VMEM((2, MESSAGE, 128), F32),
            pltpu.VMEM((2, MESSAGE, 128), F32),
            pltpu.VMEM((INNER, 128), F32),
            pltpu.VMEM((2, 24, 128), F32),
            pltpu.VMEM((PLANES, ROWS, 128), F32),
            pltpu.VMEM((POT, ROWS, 128), F32),
            pltpu.VMEM((PLANES, ROWS, 128), F32),
            pltpu.VMEM((PLANES, CROSS, 128), F32),
            pltpu.VMEM((2, PLANES, 48, 128), F32),
            pltpu.VMEM((2, PLANES, 24, 128), F32),
            pltpu.VMEM((OWN, INNER, 128), F32),
            pltpu.VMEM((OWN, 2 * INNER, 128), F32),
            pltpu.VMEM((6, INNER, 128), F32),
            pltpu.VMEM((6, INNER, 128), F32),
            dma((4,)),
            dma((2, 3)), dma((2, 3)), dma((2, 4)), dma((2, 4)), dma((2, 4)), dma((2, 4)),
            dma((2, 2)), dma((2, 2)), dma((6,)), dma((6,)), dma((2,)), dma((2,)),
        ],
        compiler_params=pltpu.CompilerParams(
            collective_id=0, has_side_effects=True, vmem_limit_bytes=60 * 1024 * 1024
        ),
    )(orbitals, potential, kinetic, gradient, *tables)
    basis = jnp.concatenate([packed[:, :, :ORB], packed[:, :, ORB:]], axis=0).reshape(CELLS, CELLS, CELLS, ORB)
    return basis, blocks[None, None, None]


def solution(mesh):
    return jax.shard_map(
        on_device,
        mesh=mesh,
        in_specs=(P("gx", "gy", "gz", None), P("gx", "gy", "gz")),
        out_specs=(P("gx", "gy", "gz", None), P("gx", "gy", "gz", None, None, None)),
        check_vma=False,
    )
```
